32 devices in a mesh: pts: 16 (over z, y, x), blk: 2 (over core).
Axes of the slice: x: 2, y: 2, z: 4, core: 2. Of those that a mesh axis runs over, the one named last changes fastest.
Arguments:
- basis_values: bfloat16 [64, 4096, 512], P(('pts', 'blk')), may hold values from -6 to 6
- density: bfloat16 [8192, 1536], P(('pts', 'blk')), may hold values from -0.01171875 to 0.01171875
- sig_blocks: int32 [64, 4], P(('pts', 'blk')), may hold values from 0 to 63, as said below
- grid_weights: float32 [64, 4096], P(('pts', 'blk')), may hold values from 0.002 to 0.02
- atom_of: int32 [64, 4096], P(('pts', 'blk')), may hold values from 0 to 511, as said below
- in_weight: float32 [256], replicated, may hold values from -4 to 4
- in_bias: float32 [256], replicated, may hold values from -3 to 3
- atom_proj: bfloat16 [256, 64], replicated, may hold values from -0.375 to 0.375
- hidden_weight: bfloat16 [256, 256], replicated, may hold values from -0.375 to 0.375
- atom_in: bfloat16 [64, 256], replicated, may hold values from -0.75 to 0.75
- hidden_bias: float32 [256], replicated, may hold values from -3 to 3
- out_weight: bfloat16 [256], replicated, may hold values from -0.375 to 0.375
Outputs:
- potential: float32 [8192, 1536], P(('pts', 'blk'))
The draws below stay inside these ranges and needn't reach their ends.
Inputs may be any that keep to these rules, and one draw needn't show every extreme that they name: `sig_blocks`: batch b lies on chip c = b // 4; its 4 blocks are distinct and lie in blocks 4 * (c - 1) to 4 * (c + 2) - 1. `atom_of`: every point of batch b, on chip c = b // 4, belongs to one of atoms 32 * (c - 1) to 32 * (c + 2) - 1.
All inputs are finite; a program needn't handle non-finite values.
Results may differ from the reference program's by a relative error of at most 0.0034.
Values may be sent and summed in bfloat16 or wider, within the bound.
A program may use at most 128 MiB of HBM per device.

```python
import math
import jax
import jax.numpy as jnp
from jax import lax

FB = 128
SIGB = 4
PTS_B = 4096
HID = 256
ATW = 64
SIGF = 512
CHIPB = 4
WINF = 1536
NB = 64
NFUNC = 8192
NBATCH = 64
BPC = 4
CHIPA = 32
NATOM = 512


def draw_sig_blocks(key, part):
    chip_of = jnp.arange(NBATCH, dtype=jnp.int32) // BPC
    offsets = jnp.arange(3 * CHIPB, dtype=jnp.int32)
    candidates = CHIPB * (chip_of[:, None] - 1) + offsets[None, :]
    inside = (candidates >= 0) & (candidates < NB)
    scores = jax.random.randint(jax.random.fold_in(key, 11), (NBATCH, 3 * CHIPB), 0, 2 ** 20) * 64 + offsets[None, :]
    scores = scores + jnp.where(inside, 0, 2 ** 28)
    order = jnp.argsort(scores, axis=1)
    picked = jnp.take_along_axis(candidates, order[:, :SIGB], axis=1)
    return picked.astype(jnp.int32)


def draw_atom_of(key, part):
    chip_of = jnp.arange(NBATCH, dtype=jnp.int32) // BPC
    lowest = jnp.maximum(CHIPA * (chip_of - 1), 0)
    highest = jnp.minimum(CHIPA * (chip_of + 2), NATOM)
    lowest = jnp.broadcast_to(lowest[:, None], (NBATCH, PTS_B))
    highest = jnp.broadcast_to(highest[:, None], (NBATCH, PTS_B))
    return jax.random.randint(jax.random.fold_in(key, 23), (NBATCH, PTS_B), lowest, highest).astype(jnp.int32)


def block_levels(key, dims, pieces, smallest, top_value):
    def one(position, shards_of):
        heights = jax.random.uniform(jax.random.fold_in(jax.random.fold_in(key, 6), position), (shards_of,), jnp.float32, smallest / len(pieces), top_value / len(pieces))
        return jnp.repeat(jnp.exp(heights), dims[position] // shards_of).reshape((-1,) + (1,) * (len(dims) - position - 1))

    factor_of = one(*pieces[0])
    for cut in pieces[1:]:
        factor_of = factor_of * one(*cut)
    return factor_of


def centred(own_key, extent, deviation, limit, shards=(), kind=jnp.bfloat16):
    entries = deviation * jax.random.normal(own_key, extent, jnp.float32)
    if shards:
        entries = entries * block_levels(own_key, extent, shards, -0.22, 0.18)
    return jnp.clip(entries, -limit, limit).astype(kind)


def setup_inputs(seed: int = 0) -> dict:
    key_list = jax.random.split(jax.random.key(seed), 13)
    basis_values = centred(key_list[0], (NBATCH, PTS_B, SIGF), 1.0, 6.0, ((0, 32),))
    density = centred(key_list[1], (NFUNC, WINF), (SIGF * SIGF) ** -0.5, 0.01171875, ((0, 32),))
    sig_blocks = draw_sig_blocks(jax.random.fold_in(key_list[12], 71), 0)
    grid_weights = jnp.clip(jnp.exp(math.log(0.02) - 2.30258502 * jax.random.uniform(key_list[3], (NBATCH, PTS_B), jnp.float32) ** block_levels(key_list[3], (NBATCH, PTS_B), ((0, 32),), -0.2, 0.2)), 0.002, 0.02)
    atom_of = draw_atom_of(jax.random.fold_in(key_list[12], 71), 0)
    in_weight = centred(key_list[5], (HID,), 1.0, 4.0, (), jnp.float32)
    in_bias = centred(key_list[6], (HID,), 0.5, 3.0, (), jnp.float32)
    atom_proj = centred(key_list[7], (HID, ATW), HID ** -0.5, 0.375)
    hidden_weight = centred(key_list[8], (HID, HID), HID ** -0.5, 0.375)
    atom_in = centred(key_list[9], (ATW, HID), ATW ** -0.5, 0.75)
    hidden_bias = centred(key_list[10], (HID,), 0.5, 3.0, (), jnp.float32)
    out_weight = centred(key_list[11], (HID,), HID ** -0.5, 0.375)
    return dict(basis_values=basis_values, density=density, sig_blocks=sig_blocks, grid_weights=grid_weights, atom_of=atom_of, in_weight=in_weight, in_bias=in_bias, atom_proj=atom_proj, hidden_weight=hidden_weight, atom_in=atom_in, hidden_bias=hidden_bias, out_weight=out_weight)


eps_atom = 0.0001

def batch_density(density, blocks):
    chip_of = blocks // CHIPB
    row_parts = []
    for row_slot in range(SIGB):
        col_parts = []
        for col_slot in range(SIGB):
            start_col = blocks[col_slot] - CHIPB * (chip_of[row_slot] - 1)
            inside = jnp.abs(chip_of[col_slot] - chip_of[row_slot]) <= 1
            start_col = jnp.clip(start_col, 0, 3 * CHIPB - 1)
            block_val = lax.dynamic_slice(density, ((blocks[row_slot] * FB).astype(jnp.int32), (start_col * FB).astype(jnp.int32)), (FB, FB))
            col_parts.append(jnp.where(inside, block_val, jnp.zeros_like(block_val)))
        row_parts.append(jnp.concatenate(col_parts, axis=1))
    return jnp.concatenate(row_parts, axis=0)

def point_hidden(rho, in_weight, in_bias):
    return jax.nn.silu(rho[:, None] * in_weight[None, :] + in_bias[None, :]).astype(jnp.bfloat16)

def reference(basis_values, density, sig_blocks, grid_weights, atom_of, in_weight, in_bias, atom_proj, hidden_weight, atom_in, hidden_bias, out_weight):

    def first_pass(carry, inputs):
        sums_acc, squares_acc = carry
        values, blocks, weights, atoms = inputs
        sub = batch_density(density, blocks)
        mixed = jnp.dot(values, sub, preferred_element_type=jnp.float32)
        rho = lax.optimization_barrier(jnp.sum(mixed * values.astype(jnp.float32), axis=1))
        hidden = point_hidden(rho, in_weight, in_bias)
        proj = jnp.dot(hidden, atom_proj, preferred_element_type=jnp.float32)
        sums_acc = sums_acc + jax.ops.segment_sum(weights[:, None] * proj, atoms, num_segments=NATOM)
        squares_acc = squares_acc + jax.ops.segment_sum(weights * weights, atoms, num_segments=NATOM)
        return ((sums_acc, squares_acc), rho)
    start = (jnp.zeros((NATOM, ATW), jnp.float32), jnp.zeros((NATOM,), jnp.float32))
    (atom_sums, atom_squares), rho_all = lax.scan(first_pass, start, (basis_values, sig_blocks, grid_weights, atom_of))
    atom_feature = (atom_sums / jnp.sqrt(atom_squares + eps_atom)[:, None]).astype(jnp.bfloat16)

    def second_pass(total, inputs):
        values, blocks, weights, atoms, rho = inputs
        hidden = point_hidden(rho, in_weight, in_bias)
        near_feature = atom_feature[atoms]
        before = jnp.dot(hidden, hidden_weight, preferred_element_type=jnp.float32) + jnp.dot(near_feature, atom_in, preferred_element_type=jnp.float32) + hidden_bias[None, :]
        second = jax.nn.silu(before).astype(jnp.bfloat16)
        point_potential = jnp.dot(second, out_weight, preferred_element_type=jnp.float32)
        weighted = ((weights * point_potential)[:, None] * values.astype(jnp.float32)).astype(jnp.bfloat16)
        batch_matrix = lax.dot_general(values, weighted, (((0,), (0,)), ((), ())), preferred_element_type=jnp.float32)
        chip_of = blocks // CHIPB
        for row_slot in range(SIGB):
            for col_slot in range(SIGB):
                start_col = blocks[col_slot] - CHIPB * (chip_of[row_slot] - 1)
                inside = jnp.abs(chip_of[col_slot] - chip_of[row_slot]) <= 1
                start_col = jnp.clip(start_col, 0, 3 * CHIPB - 1)
                block_val = batch_matrix[row_slot * FB:(row_slot + 1) * FB, col_slot * FB:(col_slot + 1) * FB]
                block_val = jnp.where(inside, block_val, jnp.zeros_like(block_val))
                corner = ((blocks[row_slot] * FB).astype(jnp.int32), (start_col * FB).astype(jnp.int32))
                current = lax.dynamic_slice(total, corner, (FB, FB))
                total = lax.dynamic_update_slice(total, current + block_val, corner)
        return (total, None)
    potential, _ = lax.scan(second_pass, jnp.zeros((NFUNC, WINF), jnp.float32), (basis_values, sig_blocks, grid_weights, atom_of, rho_all))
    return potential
```

```python
import jax
import jax.numpy as jnp
from jax import lax
from jax.experimental import pallas as pl
from jax.experimental.pallas import tpu as pltpu
from jax.sharding import PartitionSpec as P

FB = 128
ATOM_DEV = 16
eps_atom = 0.0001
f32 = jnp.float32
bf16 = jnp.bfloat16
NT = (((1,), (1,)), ((), ()))
WHOLE = pl.BlockSpec(memory_space=pltpu.VMEM)
SMALL = pl.BlockSpec(memory_space=pltpu.SMEM)


def column(row):
    return jnp.broadcast_to(row, (FB, row.shape[1])).T[:, 0:1]


def silu(v):
    half = 0.5 * v
    return half + half * jnp.tanh(half)


def members(atoms, first, count):
    ids = lax.broadcasted_iota(jnp.int32, (count, atoms.shape[1]), 0) + first
    return ids == atoms


def first_kernel(
    step_pts, own_blocks, cores,
    sig_ref, mine_ref, mate_ref, left_mine, left_mate, right_mine, right_mate,
    v_ref, w_ref, atom_ref, win_ref, bin_ref, proj_ref,
    vt_ref, hid_ref, sums_ref,
    sub_ref, seg_ref, sq_ref,
):
    batch, step = pl.program_id(0), pl.program_id(1)
    chip, core = lax.axis_index("pts"), lax.axis_index("blk")
    chip_blocks = own_blocks * cores
    count = sq_ref.shape[0]
    sig = sub_ref.shape[0] // FB

    @pl.when(step == 0)
    def _():
        for r in range(sig):
            rb = sig_ref[batch, r] - chip_blocks * (chip - 1)
            r_chip, r_in = rb // chip_blocks, rb % chip_blocks
            is_mine = (r_in // own_blocks) == core
            rows = pl.ds(pl.multiple_of((r_in % own_blocks) * FB, FB), FB)
            for s in range(sig):
                cb = sig_ref[batch, s] - chip_blocks * (chip - 1)
                c_chip = cb // chip_blocks
                low = pl.ds(pl.multiple_of(jnp.minimum(cb, 2 * chip_blocks - 1) * FB, FB), FB)
                mid = pl.ds(pl.multiple_of(cb * FB, FB), FB)
                high = pl.ds(pl.multiple_of(jnp.maximum(cb - chip_blocks, 0) * FB, FB), FB)
                left = jnp.where(is_mine, left_mine[rows, low], left_mate[rows, low])
                own = jnp.where(is_mine, mine_ref[rows, mid], mate_ref[rows, mid])
                right = jnp.where(is_mine, right_mine[rows, high], right_mate[rows, high])
                block = jnp.where(r_chip == 0, left, jnp.where(r_chip == 1, own, right))
                inside = jnp.abs(c_chip - r_chip) <= 1
                block = jnp.where(inside, block, jnp.zeros_like(block))
                sub_ref[s * FB:(s + 1) * FB, r * FB:(r + 1) * FB] = block.T

    @pl.when((step == 0) & (batch == 0))
    def _():
        seg_ref[...] = jnp.zeros_like(seg_ref)
        sq_ref[...] = jnp.zeros_like(sq_ref)

    w_in, b_in = column(win_ref[...]), column(bin_ref[...])
    first = (chip - 1) * (count // 3)
    for at in range(0, v_ref.shape[1], step_pts):
        pts = pl.ds(at, step_pts)
        vt = v_ref[0, pts, :].T
        vt_ref[0, :, pts] = vt
        mixed = jnp.dot(sub_ref[...], vt, preferred_element_type=f32)
        rho = jnp.sum(mixed * vt.astype(f32), axis=0, keepdims=True)
        hidden = silu(w_in * rho + b_in).astype(bf16)
        hid_ref[0, :, pts] = hidden
        weights = w_ref[pl.ds(batch, 1), pts]
        member = members(atom_ref[pl.ds(batch, 1), pts], first, count)
        held = jnp.where(member, jnp.broadcast_to(weights, member.shape), 0.0)
        high = held.astype(bf16)
        low = (held - high.astype(f32)).astype(bf16)
        both = jnp.concatenate([high, low], axis=0)
        seg_ref[...] += lax.dot_general(both, hidden, NT, preferred_element_type=f32)
        squares = held * held
        part = squares[:, 0:FB]
        for k in range(FB, step_pts, FB):
            part = part + squares[:, k:k + FB]
        sq_ref[...] += part

    @pl.when((step == pl.num_programs(1) - 1) & (batch == pl.num_programs(0) - 1))
    def _():
        total = seg_ref[0:count, :] + seg_ref[count:, :]
        top = total.astype(bf16)
        rest = total - top.astype(f32)
        mid = rest.astype(bf16)
        last = (rest - mid.astype(f32)).astype(bf16)
        sums = jnp.zeros((count, proj_ref.shape[1]), f32)
        for part in (last, mid, top):
            sums = sums + jnp.dot(part, proj_ref[...], preferred_element_type=f32)
        squares = jnp.sum(sq_ref[...], axis=1, keepdims=True)
        width = sums_ref.shape[1] - sums.shape[1]
        sums_ref[...] = jnp.concatenate([sums, jnp.broadcast_to(squares, (count, width))], axis=1)


def second_kernel(
    step_pts, own_blocks, cores,
    sig_ref, near_ref, vt_ref, hid_ref, w_ref, atom_ref, atin_ref, hw_ref, hb_ref, ow_ref,
    keep_ref, give_ref,
    table_ref, hwt_ref, bm_ref, acc_ref,
):
    batch, step = pl.program_id(0), pl.program_id(1)
    chip, core = lax.axis_index("pts"), lax.axis_index("blk")
    chip_blocks = own_blocks * cores
    count = near_ref.shape[0]
    width = atin_ref.shape[0]
    sig = bm_ref.shape[0] // FB

    @pl.when((step == 0) & (batch == 0))
    def _():
        squares = near_ref[:, width:width + 1]
        feature = (near_ref[:, 0:width] / jnp.sqrt(squares + eps_atom)).astype(bf16)
        table = jnp.dot(feature, atin_ref[...], preferred_element_type=f32)
        high = table.astype(bf16)
        low = (table - high.astype(f32)).astype(bf16)
        table_ref[...] = jnp.concatenate([high, low], axis=0).astype(f32).T.astype(bf16)
        hwt_ref[...] = hw_ref[...].T
        acc_ref[...] = jnp.zeros_like(acc_ref)

    @pl.when(step == 0)
    def _():
        bm_ref[...] = jnp.zeros_like(bm_ref)

    hb, ow = column(hb_ref[...]), column(ow_ref[...].astype(f32))
    first = (chip - 1) * (count // 3)
    for at in range(0, vt_ref.shape[2], step_pts):
        pts = pl.ds(at, step_pts)
        member = members(atom_ref[pl.ds(batch, 1), pts], first, count)
        member = jnp.where(member, 1.0, 0.0).astype(bf16)
        both = jnp.concatenate([member, member], axis=0)
        before = (
            jnp.dot(hwt_ref[...], hid_ref[0, :, pts], preferred_element_type=f32)
            + jnp.dot(table_ref[...], both, preferred_element_type=f32)
            + hb
        )
        second = silu(before).astype(bf16).astype(f32)
        point = jnp.sum(second * ow, axis=0, keepdims=True)
        scale = w_ref[pl.ds(batch, 1), pts] * point
        vt = vt_ref[0, :, pts]
        weighted = (scale * vt.astype(f32)).astype(bf16)
        bm_ref[...] += lax.dot_general(vt, weighted, NT, preferred_element_type=f32)

    @pl.when(step == pl.num_programs(1) - 1)
    def _():
        for r in range(sig):
            rb = sig_ref[batch, r] - chip_blocks * (chip - 1)
            r_chip, r_in = rb // chip_blocks, rb % chip_blocks
            r_core = r_in // own_blocks
            rows = pl.ds(pl.multiple_of((r_in % own_blocks) * FB, FB), FB)
            base = jnp.where(r_chip == 0, 0, jnp.where(r_chip == 1, 2 * chip_blocks, 4 * chip_blocks))
            for s in range(sig):
                cb = sig_ref[batch, s] - chip_blocks * (chip - 1)
                inside = jnp.abs(cb // chip_blocks - r_chip) <= 1

                @pl.when(inside)
                def _():
                    cols = pl.ds(pl.multiple_of((base + cb) * FB, FB), FB)
                    acc_ref[r_core, rows, cols] += bm_ref[r * FB:(r + 1) * FB, s * FB:(s + 1) * FB]

    @pl.when((step == pl.num_programs(1) - 1) & (batch == pl.num_programs(0) - 1))
    def _():
        keep_ref[...] = acc_ref[core]
        give_ref[...] = acc_ref[1 - core].astype(bf16)


def on_device(
    basis_values, density, sig_blocks, grid_weights, atom_of, in_weight, in_bias,
    atom_proj, hidden_weight, atom_in, hidden_bias, out_weight,
):
    chips, cores = lax.axis_size("pts"), lax.axis_size("blk")
    batches, points, sig = basis_values.shape
    rows, cols = density.shape
    own_blocks = rows // FB
    chip_funcs = rows * cores
    hid = in_weight.shape[0]
    width = atom_proj.shape[1]
    count = 3 * ATOM_DEV * cores
    up = [(i, i + 1) for i in range(chips - 1)]
    down = [(i + 1, i) for i in range(chips - 1)]
    swap = [(i, cores - 1 - i) for i in range(cores)]

    mate = lax.ppermute(density, "blk", swap)
    left_mine = lax.ppermute(density[:, chip_funcs:], "pts", up)
    right_mine = lax.ppermute(density[:, :2 * chip_funcs], "pts", down)
    left_mate = lax.ppermute(left_mine, "blk", swap)
    right_mate = lax.ppermute(right_mine, "blk", swap)

    block_pts = min(2048, points)
    step_pts = min(512, block_pts)
    grid = (batches, points // block_pts)
    flat = pl.BlockSpec((batches, block_pts), lambda b, i: (0, i))
    vt_spec = pl.BlockSpec((1, sig, block_pts), lambda b, i: (b, 0, i))
    hid_spec = pl.BlockSpec((1, hid, block_pts), lambda b, i: (b, 0, i))
    limit = pltpu.CompilerParams(vmem_limit_bytes=60 * 1024 * 1024)

    def first_body(*refs):
        first_kernel(step_pts, own_blocks, cores, *refs)

    vt, hidden, sums = pl.pallas_call(
        first_body,
        grid=grid,
        in_specs=[SMALL] + [WHOLE] * 6
        + [pl.BlockSpec((1, block_pts, sig), lambda b, i: (b, i, 0)), flat, flat]
        + [WHOLE] * 3,
        out_specs=[vt_spec, hid_spec, WHOLE],
        out_shape=[
            jax.ShapeDtypeStruct((batches, sig, points), bf16),
            jax.ShapeDtypeStruct((batches, hid, points), bf16),
            jax.ShapeDtypeStruct((count, 2 * width), f32),
        ],
        scratch_shapes=[
            pltpu.VMEM((sig, sig), bf16),
            pltpu.VMEM((2 * count, hid), f32),
            pltpu.VMEM((count, FB), f32),
        ],
        compiler_params=limit,
        name="first_pass",
    )(
        sig_blocks, density, mate, left_mine, left_mate, right_mine, right_mate,
        basis_values, grid_weights, atom_of, in_weight[None, :], in_bias[None, :], atom_proj,
    )

    third = count // 3
    chip_sums = sums + lax.ppermute(sums, "blk", swap)
    own = (
        chip_sums[third:2 * third]
        + lax.ppermute(chip_sums[2 * third:], "pts", up)
        + lax.ppermute(chip_sums[:third], "pts", down)
    )
    near = jnp.concatenate(
        [lax.ppermute(own, "pts", up), own, lax.ppermute(own, "pts", down)], axis=0
    )

    def second_body(*refs):
        second_kernel(step_pts, own_blocks, cores, *refs)

    packed = cols + 4 * chip_funcs
    keep, give = pl.pallas_call(
        second_body,
        grid=grid,
        in_specs=[SMALL, WHOLE, vt_spec, hid_spec, flat, flat] + [WHOLE] * 4,
        out_specs=[WHOLE, WHOLE],
        out_shape=[
            jax.ShapeDtypeStruct((rows, packed), f32),
            jax.ShapeDtypeStruct((rows, packed), bf16),
        ],
        scratch_shapes=[
            pltpu.VMEM((hid, 2 * count), bf16),
            pltpu.VMEM((hid, hid), bf16),
            pltpu.VMEM((sig, sig), f32),
            pltpu.VMEM((cores, rows, packed), f32),
        ],
        compiler_params=limit,
        name="second_pass",
    )(
        sig_blocks, near, vt, hidden, grid_weights, atom_of, atom_in, hidden_weight,
        hidden_bias[None, :], out_weight[None, :],
    )
    side = 2 * chip_funcs
    total = keep + lax.ppermute(give, "blk", swap).astype(f32)
    from_right = lax.ppermute(total[:, :side].astype(bf16), "pts", down).astype(f32)
    from_left = lax.ppermute(total[:, side + cols:].astype(bf16), "pts", up).astype(f32)
    pad = cols - side
    return (
        total[:, side:side + cols]
        + jnp.pad(from_left, ((0, 0), (0, pad)))
        + jnp.pad(from_right, ((0, 0), (pad, 0)))
    )


def solution(mesh):
    split = ("pts", "blk")
    return jax.shard_map(
        on_device,
        mesh=mesh,
        in_specs=(
            P(split, None, None), P(split, None), P(split, None), P(split, None), P(split, None),
            P(), P(), P(), P(), P(), P(), P(),
        ),
        out_specs=P(split, None),
        check_vma=False,
    )
```

```python
import jax
import jax.numpy as jnp
from jax import lax
from jax.experimental import pallas as pl
from jax.experimental.pallas import tpu as pltpu
from jax.sharding import PartitionSpec as P

FB = 128
ATOM_DEV = 16
eps_atom = 0.0001
f32 = jnp.float32
bf16 = jnp.bfloat16
NT = (((1,), (1,)), ((), ()))
WHOLE = pl.BlockSpec(memory_space=pltpu.VMEM)
SMALL = pl.BlockSpec(memory_space=pltpu.SMEM)


def column(row):
    return jnp.broadcast_to(row, (FB, row.shape[1])).T[:, 0:1]


def silu(v):
    half = 0.5 * v
    return half + half * jnp.tanh(half)


def members(atoms, first, count):
    ids = lax.broadcasted_iota(jnp.int32, (count, atoms.shape[1]), 0) + first
    return ids == atoms


def first_kernel(
    step_pts, own_blocks, cores,
    sig_ref, mine_ref, mate_ref, near_mine, near_mate, far_mine, far_mate,
    vt_ref, w_ref, atom_ref, win_ref, bin_ref, proj_ref,
    hid_ref, sums_ref,
    sub_ref, seg_ref, sq_ref,
):
    batch, step = pl.program_id(0), pl.program_id(1)
    chip, core = lax.axis_index("pts"), lax.axis_index("blk")
    chip_blocks = own_blocks * cores
    count = sq_ref.shape[0]
    sig = sub_ref.shape[0] // FB
    odd = chip % 2

    @pl.when(step == 0)
    def _():
        for r in range(sig):
            rb = sig_ref[batch, r] - chip_blocks * (chip - 1)
            r_chip, r_in = rb // chip_blocks, rb % chip_blocks
            is_mine = (r_in // own_blocks) == core
            rows = pl.ds(pl.multiple_of((r_in % own_blocks) * FB, FB), FB)
            for s in range(sig):
                cb = sig_ref[batch, s] - chip_blocks * (chip - 1)
                c_chip = cb // chip_blocks
                near_at = jnp.clip(cb + chip_blocks * (2 * odd - 1), 0, 3 * chip_blocks - 1)
                far_at = jnp.clip(cb - chip_blocks * odd, 0, 2 * chip_blocks - 1)
                mid = pl.ds(pl.multiple_of(cb * FB, FB), FB)
                near = pl.ds(pl.multiple_of(near_at * FB, FB), FB)
                far = pl.ds(pl.multiple_of(far_at * FB, FB), FB)
                block = jnp.where(
                    r_chip == 1,
                    jnp.where(is_mine, mine_ref[rows, mid], mate_ref[rows, mid]),
                    jnp.where(
                        r_chip == 2 - 2 * odd,
                        jnp.where(is_mine, near_mine[rows, near], near_mate[rows, near]),
                        jnp.where(is_mine, far_mine[rows, far], far_mate[rows, far]),
                    ),
                )
                inside = jnp.abs(c_chip - r_chip) <= 1
                block = jnp.where(inside, block, jnp.zeros_like(block))
                sub_ref[s * FB:(s + 1) * FB, r * FB:(r + 1) * FB] = block.T

    @pl.when((step == 0) & (batch == 0))
    def _():
        seg_ref[...] = jnp.zeros_like(seg_ref)
        sq_ref[...] = jnp.zeros_like(sq_ref)

    w_in, b_in = column(win_ref[...]), column(bin_ref[...])
    first = (chip - 1) * (count // 3)
    for at in range(0, vt_ref.shape[2], step_pts):
        pts = pl.ds(at, step_pts)
        vt = vt_ref[0, :, pts]
        mixed = jnp.dot(sub_ref[...], vt, preferred_element_type=f32)
        rho = jnp.sum(mixed * vt.astype(f32), axis=0, keepdims=True)
        hidden = silu(w_in * rho + b_in).astype(bf16)
        hid_ref[0, :, pts] = hidden
        weights = w_ref[pl.ds(batch, 1), pts]
        member = members(atom_ref[pl.ds(batch, 1), pts], first, count)
        held = jnp.where(member, jnp.broadcast_to(weights, member.shape), 0.0)
        high = held.astype(bf16)
        low = (held - high.astype(f32)).astype(bf16)
        both = jnp.concatenate([high, low], axis=0)
        seg_ref[...] += lax.dot_general(both, hidden, NT, preferred_element_type=f32)
        squares = held * held
        part = squares[:, 0:FB]
        for k in range(FB, step_pts, FB):
            part = part + squares[:, k:k + FB]
        sq_ref[...] += part

    @pl.when((step == pl.num_programs(1) - 1) & (batch == pl.num_programs(0) - 1))
    def _():
        total = seg_ref[0:count, :] + seg_ref[count:, :]
        top = total.astype(bf16)
        rest = total - top.astype(f32)
        mid = rest.astype(bf16)
        last = (rest - mid.astype(f32)).astype(bf16)
        sums = jnp.zeros((count, proj_ref.shape[1]), f32)
        for part in (last, mid, top):
            sums = sums + jnp.dot(part, proj_ref[...], preferred_element_type=f32)
        squares = jnp.sum(sq_ref[...], axis=1, keepdims=True)
        width = sums_ref.shape[1] - sums.shape[1]
        sums_ref[...] = jnp.concatenate([sums, jnp.broadcast_to(squares, (count, width))], axis=1)


def second_kernel(
    step_pts, own_blocks, cores,
    sig_ref, near_ref, vt_ref, hid_ref, w_ref, atom_ref, atin_ref, hw_ref, hb_ref, ow_ref,
    keep_ref, give_ref,
    table_ref, hwt_ref, bm_ref, acc_ref,
):
    batch, step = pl.program_id(0), pl.program_id(1)
    chip, core = lax.axis_index("pts"), lax.axis_index("blk")
    chip_blocks = own_blocks * cores
    count = near_ref.shape[0]
    width = atin_ref.shape[0]
    sig = bm_ref.shape[0] // FB

    @pl.when((step == 0) & (batch == 0))
    def _():
        squares = near_ref[:, width:width + 1]
        feature = (near_ref[:, 0:width] / jnp.sqrt(squares + eps_atom)).astype(bf16)
        table = jnp.dot(feature, atin_ref[...], preferred_element_type=f32)
        high = table.astype(bf16)
        low = (table - high.astype(f32)).astype(bf16)
        table_ref[...] = jnp.concatenate([high, low], axis=0).astype(f32).T.astype(bf16)
        hwt_ref[...] = hw_ref[...].T
        acc_ref[...] = jnp.zeros_like(acc_ref)

    @pl.when(step == 0)
    def _():
        bm_ref[...] = jnp.zeros_like(bm_ref)

    hb, ow = column(hb_ref[...]), column(ow_ref[...].astype(f32))
    first = (chip - 1) * (count // 3)
    for at in range(0, vt_ref.shape[2], step_pts):
        pts = pl.ds(at, step_pts)
        member = members(atom_ref[pl.ds(batch, 1), pts], first, count)
        member = jnp.where(member, 1.0, 0.0).astype(bf16)
        both = jnp.concatenate([member, member], axis=0)
        before = (
            jnp.dot(hwt_ref[...], hid_ref[0, :, pts], preferred_element_type=f32)
            + jnp.dot(table_ref[...], both, preferred_element_type=f32)
            + hb
        )
        second = silu(before).astype(bf16).astype(f32)
        point = jnp.sum(second * ow, axis=0, keepdims=True)
        scale = w_ref[pl.ds(batch, 1), pts] * point
        vt = vt_ref[0, :, pts]
        weighted = (scale * vt.astype(f32)).astype(bf16)
        bm_ref[...] += lax.dot_general(vt, weighted, NT, preferred_element_type=f32)

    @pl.when(step == pl.num_programs(1) - 1)
    def _():
        for r in range(sig):
            rb = sig_ref[batch, r] - chip_blocks * (chip - 1)
            r_chip, r_in = rb // chip_blocks, rb % chip_blocks
            r_core = r_in // own_blocks
            rows = pl.ds(pl.multiple_of((r_in % own_blocks) * FB, FB), FB)
            base = jnp.where(r_chip == 0, 0, jnp.where(r_chip == 1, 2 * chip_blocks, 4 * chip_blocks))
            for s in range(sig):
                cb = sig_ref[batch, s] - chip_blocks * (chip - 1)
                inside = jnp.abs(cb // chip_blocks - r_chip) <= 1

                @pl.when(inside)
                def _():
                    cols = pl.ds(pl.multiple_of((base + cb) * FB, FB), FB)
                    acc_ref[r_core, rows, cols] += bm_ref[r * FB:(r + 1) * FB, s * FB:(s + 1) * FB]

    @pl.when((step == pl.num_programs(1) - 1) & (batch == pl.num_programs(0) - 1))
    def _():
        keep_ref[...] = acc_ref[core]
        give_ref[...] = acc_ref[1 - core].astype(bf16)


def remote(src, dst, send, recv, chip, core):
    return pltpu.make_async_remote_copy(
        src_ref=src, dst_ref=dst, send_sem=send, recv_sem=recv,
        device_id=(chip, core), device_id_type=pl.DeviceIdType.MESH,
    )


def greet(peers):
    barrier = pltpu.get_barrier_semaphore()
    for exists, chip, core in peers:
        @pl.when(exists)
        def _():
            pl.semaphore_signal(
                barrier, inc=1, device_id=(chip, core), device_id_type=pl.DeviceIdType.MESH
            )
    pl.semaphore_wait(barrier, sum(jnp.where(exists, 1, 0) for exists, _, _ in peers))


def gather_kernel(
    chips, side, pieces,
    dens_ref, v_ref,
    vt_ref, mate_ref, near_ref, near_mate, far_ref, far_mate,
    near_s, near_r, mate_s, mate_r, relay_s, relay_r, fwd_s, fwd_r, last_s, last_r,
):
    step, steps = pl.program_id(0), pl.num_programs(0)
    chip, core = lax.axis_index("pts"), lax.axis_index("blk")
    odd = chip % 2
    partner = chip + 1 - 2 * odd
    ahead = chip + 2 - 4 * odd
    behind = chip - 2 + 4 * odd
    has_ahead = (ahead >= 0) & (ahead < chips)
    has_behind = (behind >= 0) & (behind < chips)
    rows = dens_ref.shape[0] // pieces
    part = pl.ds(pl.multiple_of((1 - odd) * (near_ref.shape[1] - side), FB), side)

    def cut(i):
        return pl.ds(i * rows, rows)

    def to_near(i):
        return remote(dens_ref.at[cut(i)], near_ref.at[cut(i)], near_s.at[i], near_r.at[i], partner, core)

    def to_mate():
        return remote(dens_ref, mate_ref, mate_s, mate_r, chip, 1 - core)

    def relay(i):
        return remote(near_ref.at[cut(i), part], far_ref.at[cut(i)], relay_s.at[i], relay_r.at[i], ahead, core)

    def forward(i):
        return remote(near_ref.at[cut(i)], near_mate.at[cut(i)], fwd_s.at[i], fwd_r.at[i], chip, 1 - core)

    def finish(i):
        return remote(far_ref.at[cut(i)], far_mate.at[cut(i)], last_s.at[i], last_r.at[i], chip, 1 - core)

    @pl.when(step == 0)
    def _():
        greet([
            (True, chip, 1 - core), (True, partner, core),
            (has_ahead, ahead, core), (has_behind, behind, core),
        ])
        for i in range(pieces):
            to_near(i).start()
        to_mate().start()

    vt_ref[0] = v_ref[0].T

    for i in range(pieces):
        @pl.when(step == ((i + 1) * steps) // pieces - 1)
        def _():
            to_near(i).wait_recv()

            @pl.when(has_ahead)
            def _():
                relay(i).start()

            forward(i).start()

    @pl.when(step == steps - 1)
    def _():
        for i in range(pieces):
            @pl.when(has_behind)
            def _():
                relay(i).wait_recv()
                finish(i).start()
        to_mate().wait()
        for i in range(pieces):
            to_near(i).wait_send()
            forward(i).wait()

            @pl.when(has_ahead)
            def _():
                relay(i).wait_send()

            @pl.when(has_behind)
            def _():
                finish(i).wait()


def atoms_kernel(chips, cores, sums_ref, near_ref, land_ref, send, recv):
    chip, core = lax.axis_index("pts"), lax.axis_index("blk")
    third = sums_ref.shape[0] // 3
    plans = []
    for d in (-1, 1, -2, 2):
        for flip in (0, 1):
            plans.append((d, flip))
    plans.append((0, 1))

    def other(flip):
        return core + flip * (1 - 2 * core)

    def span(d):
        count = 3 - abs(d)
        return max(d, 0), max(-d, 0), count

    def valid(at):
        return (at >= 0) & (at < chips)

    def copy(k, d, flip):
        take, _, count = span(d)
        return remote(
            sums_ref.at[pl.ds(take * third, count * third)],
            land_ref.at[k, pl.ds(0, count * third)],
            send.at[k], recv.at[k], chip + d, other(flip),
        )

    greet([(valid(chip + d), chip + d, other(flip)) for d, flip in plans])
    for k, (d, flip) in enumerate(plans):
        @pl.when(valid(chip + d))
        def _():
            copy(k, d, flip).start()

    near_ref[...] = sums_ref[...]
    for k, (d, flip) in enumerate(plans):
        _, put, count = span(d)

        @pl.when(valid(chip - d))
        def _():
            copy(k, d, flip).wait_recv()
            to = pl.ds(put * third, count * third)
            near_ref[to, :] += land_ref[k, 0:count * third, :]

    for k, (d, flip) in enumerate(plans):
        @pl.when(valid(chip + d))
        def _():
            copy(k, d, flip).wait_send()


def scatter_kernel(
    chips, side, pieces,
    keep_ref, give_ref, out_ref,
    mate_buf, total, far_out, far_in, near_out, near_in,
    mate_s, mate_r, far_s, far_r, near_s, near_r,
):
    chip, core = lax.axis_index("pts"), lax.axis_index("blk")
    odd = chip % 2
    partner = chip + 1 - 2 * odd
    ahead = chip + 2 - 4 * odd
    behind = chip - 2 + 4 * odd
    has_ahead = (ahead >= 0) & (ahead < chips)
    has_behind = (behind >= 0) & (behind < chips)
    rows = keep_ref.shape[0] // pieces
    cols = out_ref.shape[1]
    third = cols - side
    far_at = pl.multiple_of(odd * (side + cols), FB)
    near_at = pl.multiple_of((1 - odd) * (side + cols), FB)

    def cut(i):
        return pl.ds(i * rows, rows)

    def to_mate(i):
        return remote(give_ref.at[cut(i)], mate_buf.at[cut(i)], mate_s.at[i], mate_r.at[i], chip, 1 - core)

    def to_far(i):
        return remote(far_out.at[cut(i)], far_in.at[cut(i)], far_s.at[i], far_r.at[i], behind, core)

    def to_near(i):
        return remote(near_out.at[cut(i)], near_in.at[cut(i)], near_s.at[i], near_r.at[i], partner, core)

    greet([
        (True, chip, 1 - core), (True, partner, core),
        (has_ahead, ahead, core), (has_behind, behind, core),
    ])
    for i in range(pieces):
        to_mate(i).start()
    for i in range(pieces):
        to_mate(i).wait_recv()
        total[cut(i), :] = keep_ref[cut(i), :] + mate_buf[cut(i), :].astype(f32)
        far_out[cut(i), :] = total[cut(i), pl.ds(far_at, side)].astype(bf16)

        @pl.when(has_behind)
        def _():
            to_far(i).start()

    for i in range(pieces):
        @pl.when(has_ahead)
        def _():
            to_far(i).wait_recv()

        mine = total[cut(i), pl.ds(near_at, side)]
        theirs = jnp.where(has_ahead, far_in[cut(i), :].astype(f32), 0.0)
        blank = jnp.zeros((rows, third), f32)
        low = jnp.where(odd == 0, mine, theirs)
        high = jnp.where(odd == 0, theirs, mine)
        both = jnp.concatenate([low, blank], axis=1) + jnp.concatenate([blank, high], axis=1)
        near_out[cut(i), :] = both.astype(bf16)
        to_near(i).start()

    for i in range(pieces):
        to_near(i).wait_recv()
        out_ref[cut(i), :] = total[cut(i), side:side + cols] + near_in[cut(i), :].astype(f32)

    for i in range(pieces):
        to_mate(i).wait_send()
        to_near(i).wait_send()

        @pl.when(has_behind)
        def _():
            to_far(i).wait_send()


def on_device(
    basis_values, density, sig_blocks, grid_weights, atom_of, in_weight, in_bias,
    atom_proj, hidden_weight, atom_in, hidden_bias, out_weight,
):
    chips, cores = lax.axis_size("pts"), lax.axis_size("blk")
    batches, points, sig = basis_values.shape
    rows, cols = density.shape
    own_blocks = rows // FB
    chip_funcs = rows * cores
    hid = in_weight.shape[0]
    width = atom_proj.shape[1]
    count = 3 * ATOM_DEV * cores
    side = 2 * chip_funcs
    hbm = pl.BlockSpec(memory_space=pl.ANY)
    dma = pltpu.SemaphoreType.DMA

    def talk(number):
        return pltpu.CompilerParams(
            collective_id=number, has_side_effects=True, vmem_limit_bytes=40 * 1024 * 1024
        )

    pieces = 4
    turn_pts = min(1024, points)
    turns = points // turn_pts

    def gather_body(*refs):
        gather_kernel(chips, side, pieces, *refs)

    vt, mate, near_mine, near_mate, far_mine, far_mate = pl.pallas_call(
        gather_body,
        grid=(batches * turns,),
        in_specs=[hbm, pl.BlockSpec((1, turn_pts, sig), lambda g: (g // turns, g % turns, 0))],
        out_specs=[pl.BlockSpec((1, sig, turn_pts), lambda g: (g // turns, 0, g % turns))] + [hbm] * 5,
        out_shape=[jax.ShapeDtypeStruct((batches, sig, points), bf16)]
        + [jax.ShapeDtypeStruct((rows, cols), bf16)] * 3
        + [jax.ShapeDtypeStruct((rows, side), bf16)] * 2,
        scratch_shapes=[dma((pieces,)), dma((pieces,)), dma, dma] + [dma((pieces,))] * 6,
        compiler_params=talk(0),
        name="gather_density",
    )(density, basis_values)

    block_pts = min(2048, points)
    step_pts = min(512, block_pts)
    grid = (batches, points // block_pts)
    flat = pl.BlockSpec((batches, block_pts), lambda b, i: (0, i))
    vt_spec = pl.BlockSpec((1, sig, block_pts), lambda b, i: (b, 0, i))
    hid_spec = pl.BlockSpec((1, hid, block_pts), lambda b, i: (b, 0, i))
    limit = pltpu.CompilerParams(vmem_limit_bytes=60 * 1024 * 1024)

    def first_body(*refs):
        first_kernel(step_pts, own_blocks, cores, *refs)

    hidden, sums = pl.pallas_call(
        first_body,
        grid=grid,
        in_specs=[SMALL] + [WHOLE] * 6
        + [vt_spec, flat, flat]
        + [WHOLE] * 3,
        out_specs=[hid_spec, WHOLE],
        out_shape=[
            jax.ShapeDtypeStruct((batches, hid, points), bf16),
            jax.ShapeDtypeStruct((count, 2 * width), f32),
        ],
        scratch_shapes=[
            pltpu.VMEM((sig, sig), bf16),
            pltpu.VMEM((2 * count, hid), f32),
            pltpu.VMEM((count, FB), f32),
        ],
        compiler_params=limit,
        name="first_pass",
    )(
        sig_blocks, density, mate, near_mine, near_mate, far_mine, far_mate,
        vt, grid_weights, atom_of, in_weight[None, :], in_bias[None, :], atom_proj,
    )

    def atoms_body(*refs):
        atoms_kernel(chips, cores, *refs)

    near = pl.pallas_call(
        atoms_body,
        in_specs=[WHOLE],
        out_specs=WHOLE,
        out_shape=jax.ShapeDtypeStruct(sums.shape, f32),
        scratch_shapes=[pltpu.VMEM((9,) + sums.shape, f32), dma((9,)), dma((9,))],
        compiler_params=talk(1),
        name="atom_exchange",
    )(sums)

    def second_body(*refs):
        second_kernel(step_pts, own_blocks, cores, *refs)

    packed = cols + 4 * chip_funcs
    keep, give = pl.pallas_call(
        second_body,
        grid=grid,
        in_specs=[SMALL, WHOLE, vt_spec, hid_spec, flat, flat] + [WHOLE] * 4,
        out_specs=[WHOLE, WHOLE],
        out_shape=[
            jax.ShapeDtypeStruct((rows, packed), f32),
            jax.ShapeDtypeStruct((rows, packed), bf16),
        ],
        scratch_shapes=[
            pltpu.VMEM((hid, 2 * count), bf16),
            pltpu.VMEM((hid, hid), bf16),
            pltpu.VMEM((sig, sig), f32),
            pltpu.VMEM((cores, rows, packed), f32),
        ],
        compiler_params=limit,
        name="second_pass",
    )(
        sig_blocks, near, vt, hidden, grid_weights, atom_of, atom_in, hidden_weight,
        hidden_bias[None, :], out_weight[None, :],
    )

    def scatter_body(*refs):
        scatter_kernel(chips, side, pieces, *refs)

    return pl.pallas_call(
        scatter_body,
        in_specs=[WHOLE, WHOLE],
        out_specs=WHOLE,
        out_shape=jax.ShapeDtypeStruct((rows, cols), f32),
        scratch_shapes=[
            pltpu.VMEM((rows, packed), bf16),
            pltpu.VMEM((rows, packed), f32),
            pltpu.VMEM((rows, side), bf16),
            pltpu.VMEM((rows, side), bf16),
            pltpu.VMEM((rows, cols), bf16),
            pltpu.VMEM((rows, cols), bf16),
        ] + [dma((pieces,))] * 6,
        compiler_params=talk(2),
        name="scatter_terms",
    )(keep, give)


def solution(mesh):
    split = ("pts", "blk")
    return jax.shard_map(
        on_device,
        mesh=mesh,
        in_specs=(
            P(split, None, None), P(split, None), P(split, None), P(split, None), P(split, None),
            P(), P(), P(), P(), P(), P(), P(),
        ),
        out_specs=P(split, None),
        check_vma=False,
    )
```

```python
import jax
import jax.numpy as jnp
from jax import lax
from jax.experimental import pallas as pl
from jax.experimental.pallas import tpu as pltpu
from jax.sharding import PartitionSpec as P

FB = 128
ATOM_DEV = 16
eps_atom = 0.0001
f32 = jnp.float32
bf16 = jnp.bfloat16
NT = (((1,), (1,)), ((), ()))
WHOLE = pl.BlockSpec(memory_space=pltpu.VMEM)
SMALL = pl.BlockSpec(memory_space=pltpu.SMEM)


def column(row):
    return jnp.broadcast_to(row, (FB, row.shape[1])).T[:, 0:1]


def silu(v):
    half = 0.5 * v
    return half + half * jnp.tanh(half)


def members(atoms, first, count):
    ids = lax.broadcasted_iota(jnp.int32, (count, atoms.shape[1]), 0) + first
    return ids == atoms


def first_kernel(
    step_pts, own_blocks, cores,
    sig_ref, mine_ref, mate_ref, near_mine, near_mate, far_mine, far_mate,
    vt_ref, w_ref, atom_ref, win_ref, bin_ref, proj_ref,
    hid_ref, sums_ref,
    sub_ref, seg_ref, sq_ref,
):
    batch, step = pl.program_id(0), pl.program_id(1)
    chip, core = lax.axis_index("pts"), lax.axis_index("blk")
    chip_blocks = own_blocks * cores
    count = sq_ref.shape[0]
    sig = sub_ref.shape[0] // FB
    odd = chip % 2

    @pl.when(step == 0)
    def _():
        for r in range(sig):
            rb = sig_ref[batch, r] - chip_blocks * (chip - 1)
            r_chip, r_in = rb // chip_blocks, rb % chip_blocks
            is_mine = (r_in // own_blocks) == core
            rows = pl.ds(pl.multiple_of((r_in % own_blocks) * FB, FB), FB)
            for s in range(sig):
                cb = sig_ref[batch, s] - chip_blocks * (chip - 1)
                c_chip = cb // chip_blocks
                near_at = jnp.clip(cb + chip_blocks * (2 * odd - 1), 0, 3 * chip_blocks - 1)
                far_at = jnp.clip(cb - chip_blocks * odd, 0, 2 * chip_blocks - 1)
                mid = pl.ds(pl.multiple_of(cb * FB, FB), FB)
                near = pl.ds(pl.multiple_of(near_at * FB, FB), FB)
                far = pl.ds(pl.multiple_of(far_at * FB, FB), FB)
                block = jnp.where(
                    r_chip == 1,
                    jnp.where(is_mine, mine_ref[rows, mid], mate_ref[rows, mid]),
                    jnp.where(
                        r_chip == 2 - 2 * odd,
                        jnp.where(is_mine, near_mine[rows, near], near_mate[rows, near]),
                        jnp.where(is_mine, far_mine[rows, far], far_mate[rows, far]),
                    ),
                )
                inside = jnp.abs(c_chip - r_chip) <= 1
                block = jnp.where(inside, block, jnp.zeros_like(block))
                sub_ref[s * FB:(s + 1) * FB, r * FB:(r + 1) * FB] = block.T
        half = sub_ref.shape[0] // 2
        folded = sub_ref[0:half, half:].astype(f32) + sub_ref[half:, 0:half].astype(f32).T
        sub_ref[0:half, half:] = folded.astype(bf16)

    @pl.when((step == 0) & (batch == 0))
    def _():
        seg_ref[...] = jnp.zeros_like(seg_ref)
        sq_ref[...] = jnp.zeros_like(sq_ref)

    w_in, b_in = column(win_ref[...]), column(bin_ref[...])
    first = (chip - 1) * (count // 3)
    for at in range(0, vt_ref.shape[2], step_pts):
        pts = pl.ds(at, step_pts)
        vt = vt_ref[0, :, pts]
        half = sub_ref.shape[0] // 2
        mixed = jnp.dot(sub_ref[0:half, :], vt, preferred_element_type=f32)
        rho = jnp.sum(mixed * vt[0:half].astype(f32), axis=0, keepdims=True)
        mixed = jnp.dot(sub_ref[half:, half:], vt[half:], preferred_element_type=f32)
        rho = rho + jnp.sum(mixed * vt[half:].astype(f32), axis=0, keepdims=True)
        hidden = silu(w_in * rho + b_in).astype(bf16)
        hid_ref[0, :, pts] = hidden
        weights = w_ref[pl.ds(batch, 1), pts]
        member = members(atom_ref[pl.ds(batch, 1), pts], first, count)
        held = jnp.where(member, jnp.broadcast_to(weights, member.shape), 0.0)
        high = held.astype(bf16)
        low = (held - high.astype(f32)).astype(bf16)
        both = jnp.concatenate([high, low], axis=0)
        seg_ref[...] += lax.dot_general(both, hidden, NT, preferred_element_type=f32)
        squares = held * held
        part = squares[:, 0:FB]
        for k in range(FB, step_pts, FB):
            part = part + squares[:, k:k + FB]
        sq_ref[...] += part

    @pl.when((step == pl.num_programs(1) - 1) & (batch == pl.num_programs(0) - 1))
    def _():
        total = seg_ref[0:count, :] + seg_ref[count:, :]
        top = total.astype(bf16)
        rest = total - top.astype(f32)
        mid = rest.astype(bf16)
        last = (rest - mid.astype(f32)).astype(bf16)
        sums = jnp.zeros((count, proj_ref.shape[0]), f32)
        for part in (last, mid, top):
            sums = sums + lax.dot_general(part, proj_ref[...], NT, preferred_element_type=f32)
        squares = jnp.sum(sq_ref[...], axis=1, keepdims=True)
        width = sums_ref.shape[1] - sums.shape[1]
        sums_ref[...] = jnp.concatenate([sums, jnp.broadcast_to(squares, (count, width))], axis=1)


def second_kernel(
    step_pts, own_blocks, cores,
    sig_ref, near_ref, v_ref, vt_ref, hid_ref, w_ref, atom_ref, atin_ref, hw_ref, hb_ref, ow_ref,
    keep_ref, give_ref,
    table_ref, hwt_ref, bm_ref, acc_ref, wt_ref,
):
    batch, step = pl.program_id(0), pl.program_id(1)
    chip, core = lax.axis_index("pts"), lax.axis_index("blk")
    chip_blocks = own_blocks * cores
    count = near_ref.shape[0]
    width = atin_ref.shape[0]
    sig = bm_ref.shape[0] // FB

    @pl.when((step == 0) & (batch == 0))
    def _():
        squares = near_ref[:, width:width + 1]
        feature = (near_ref[:, 0:width] / jnp.sqrt(squares + eps_atom)).astype(bf16)
        table = jnp.dot(feature, atin_ref[...], preferred_element_type=f32)
        high = table.astype(bf16)
        low = (table - high.astype(f32)).astype(bf16)
        table_ref[...] = jnp.concatenate([high, low], axis=0).astype(f32).T.astype(bf16)
        hwt_ref[...] = hw_ref[...].T
        acc_ref[...] = jnp.zeros_like(acc_ref)

    @pl.when(step == 0)
    def _():
        bm_ref[...] = jnp.zeros_like(bm_ref)

    hb, ow = column(hb_ref[...]), column(ow_ref[...].astype(f32))
    first = (chip - 1) * (count // 3)
    for at in range(0, vt_ref.shape[2], step_pts):
        pts = pl.ds(at, step_pts)
        member = members(atom_ref[pl.ds(batch, 1), pts], first, count)
        member = jnp.where(member, 1.0, 0.0).astype(bf16)
        both = jnp.concatenate([member, member], axis=0)
        before = (
            jnp.dot(hwt_ref[...], hid_ref[0, :, pts], preferred_element_type=f32)
            + jnp.dot(table_ref[...], both, preferred_element_type=f32)
            + hb
        )
        second = silu(before).astype(bf16).astype(f32)
        point = jnp.sum(second * ow, axis=0, keepdims=True)
        scale = w_ref[pl.ds(batch, 1), pts] * point
        vt = vt_ref[0, :, pts]
        wt_ref[:, pts] = (scale * vt.astype(f32)).astype(bf16)

    half = bm_ref.shape[0] // 2
    bm_ref[0:half, :] += jnp.dot(wt_ref[0:half, :], v_ref[0], preferred_element_type=f32)
    bm_ref[half:, half:] += jnp.dot(wt_ref[half:, :], v_ref[0, :, half:], preferred_element_type=f32)

    @pl.when(step == pl.num_programs(1) - 1)
    def _():
        bm_ref[half:, 0:half] = bm_ref[0:half, half:].T
        for r in range(sig):
            rb = sig_ref[batch, r] - chip_blocks * (chip - 1)
            r_chip, r_in = rb // chip_blocks, rb % chip_blocks
            r_core = r_in // own_blocks
            rows = pl.ds(pl.multiple_of((r_in % own_blocks) * FB, FB), FB)
            base = jnp.where(r_chip == 0, 0, jnp.where(r_chip == 1, 2 * chip_blocks, 4 * chip_blocks))
            for s in range(sig):
                cb = sig_ref[batch, s] - chip_blocks * (chip - 1)
                inside = jnp.abs(cb // chip_blocks - r_chip) <= 1

                @pl.when(inside)
                def _():
                    cols = pl.ds(pl.multiple_of((base + cb) * FB, FB), FB)
                    acc_ref[r_core, rows, cols] += bm_ref[r * FB:(r + 1) * FB, s * FB:(s + 1) * FB]

    @pl.when((step == pl.num_programs(1) - 1) & (batch == pl.num_programs(0) - 1))
    def _():
        keep_ref[...] = acc_ref[core]
        give_ref[...] = acc_ref[1 - core].astype(bf16)


def remote(src, dst, send, recv, chip, core):
    return pltpu.make_async_remote_copy(
        src_ref=src, dst_ref=dst, send_sem=send, recv_sem=recv,
        device_id=(chip, core), device_id_type=pl.DeviceIdType.MESH,
    )


def greet(peers):
    barrier = pltpu.get_barrier_semaphore()
    for exists, chip, core in peers:
        @pl.when(exists)
        def _():
            pl.semaphore_signal(
                barrier, inc=1, device_id=(chip, core), device_id_type=pl.DeviceIdType.MESH
            )
    pl.semaphore_wait(barrier, sum(jnp.where(exists, 1, 0) for exists, _, _ in peers))


def gather_kernel(
    chips, side, pieces,
    dens_ref, v_ref,
    vt_ref, mate_ref, near_ref, near_mate, far_ref, far_mate,
    near_s, near_r, mate_s, mate_r, relay_s, relay_r, fwd_s, fwd_r, last_s, last_r,
):
    step, steps = pl.program_id(0), pl.num_programs(0)
    chip, core = lax.axis_index("pts"), lax.axis_index("blk")
    odd = chip % 2
    partner = chip + 1 - 2 * odd
    ahead = chip + 2 - 4 * odd
    behind = chip - 2 + 4 * odd
    has_ahead = (ahead >= 0) & (ahead < chips)
    has_behind = (behind >= 0) & (behind < chips)
    rows = dens_ref.shape[0] // pieces
    third = near_ref.shape[1] - side
    mine_part = pl.ds(pl.multiple_of(odd * third, FB), side)
    mine_rest = pl.ds(pl.multiple_of((1 - odd) * side, FB), third)
    part = pl.ds(pl.multiple_of((1 - odd) * third, FB), side)
    rest = pl.ds(pl.multiple_of(odd * side, FB), third)

    def cut(i):
        return pl.ds(i * rows, rows)

    def to_near(i):
        return remote(
            dens_ref.at[cut(i), mine_part], near_ref.at[cut(i), mine_part],
            near_s.at[i], near_r.at[i], partner, core,
        )

    def from_near(i):
        return remote(
            dens_ref.at[cut(i), part], near_ref.at[cut(i), part],
            near_s.at[i], near_r.at[i], partner, core,
        )

    def rest_near():
        return remote(
            dens_ref.at[:, mine_rest], near_ref.at[:, mine_rest],
            near_s.at[pieces], near_r.at[pieces], partner, core,
        )

    def rest_from():
        return remote(
            dens_ref.at[:, rest], near_ref.at[:, rest],
            near_s.at[pieces], near_r.at[pieces], partner, core,
        )

    def to_mate():
        return remote(dens_ref, mate_ref, mate_s, mate_r, chip, 1 - core)

    def relay(i):
        return remote(near_ref.at[cut(i), part], far_ref.at[cut(i)], relay_s.at[i], relay_r.at[i], ahead, core)

    def forward(i):
        return remote(near_ref.at[cut(i), part], near_mate.at[cut(i), part], fwd_s.at[i], fwd_r.at[i], chip, 1 - core)

    def rest_forward():
        return remote(
            near_ref.at[:, rest], near_mate.at[:, rest],
            fwd_s.at[pieces], fwd_r.at[pieces], chip, 1 - core,
        )

    def finish(i):
        return remote(far_ref.at[cut(i)], far_mate.at[cut(i)], last_s.at[i], last_r.at[i], chip, 1 - core)

    @pl.when(step == 0)
    def _():
        greet([
            (True, chip, 1 - core), (True, partner, core),
            (has_ahead, ahead, core), (has_behind, behind, core),
        ])
        for i in range(pieces):
            to_near(i).start()
        rest_near().start()
        to_mate().start()

    vt_ref[0] = v_ref[0].T

    for i in range(pieces):
        @pl.when(step == ((i + 1) * steps) // pieces - 1)
        def _():
            from_near(i).wait_recv()

            @pl.when(has_ahead)
            def _():
                relay(i).start()

            forward(i).start()

    @pl.when(step == steps - 1)
    def _():
        for i in range(pieces):
            @pl.when(has_behind)
            def _():
                relay(i).wait_recv()
                finish(i).start()
        rest_from().wait_recv()
        rest_forward().start()
        to_mate().wait()
        rest_near().wait_send()
        rest_forward().wait()
        for i in range(pieces):
            to_near(i).wait_send()
            forward(i).wait()

            @pl.when(has_ahead)
            def _():
                relay(i).wait_send()

            @pl.when(has_behind)
            def _():
                finish(i).wait()


def atoms_kernel(chips, cores, sums_ref, near_ref, land_ref, send, recv):
    chip, core = lax.axis_index("pts"), lax.axis_index("blk")
    third = sums_ref.shape[0] // 3
    plans = []
    for d in (-1, 1, -2, 2):
        for flip in (0, 1):
            plans.append((d, flip))
    plans.append((0, 1))

    def other(flip):
        return core + flip * (1 - 2 * core)

    def span(d):
        count = 3 - abs(d)
        return max(d, 0), max(-d, 0), count

    def valid(at):
        return (at >= 0) & (at < chips)

    def copy(k, d, flip):
        take, _, count = span(d)
        return remote(
            sums_ref.at[pl.ds(take * third, count * third)],
            land_ref.at[k, pl.ds(0, count * third)],
            send.at[k], recv.at[k], chip + d, other(flip),
        )

    greet([(valid(chip + d), chip + d, other(flip)) for d, flip in plans])
    for k, (d, flip) in enumerate(plans):
        @pl.when(valid(chip + d))
        def _():
            copy(k, d, flip).start()

    near_ref[...] = sums_ref[...]
    for k, (d, flip) in enumerate(plans):
        _, put, count = span(d)

        @pl.when(valid(chip - d))
        def _():
            copy(k, d, flip).wait_recv()
            to = pl.ds(put * third, count * third)
            near_ref[to, :] += land_ref[k, 0:count * third, :]

    for k, (d, flip) in enumerate(plans):
        @pl.when(valid(chip + d))
        def _():
            copy(k, d, flip).wait_send()


def scatter_kernel(
    chips, side, pieces,
    keep_ref, give_ref, out_ref,
    mate_buf, total, far_out, far_in, near_out, near_in,
    mate_s, mate_r, far_s, far_r, near_s, near_r, load_s,
):
    chip, core = lax.axis_index("pts"), lax.axis_index("blk")
    odd = chip % 2
    partner = chip + 1 - 2 * odd
    ahead = chip + 2 - 4 * odd
    behind = chip - 2 + 4 * odd
    has_ahead = (ahead >= 0) & (ahead < chips)
    has_behind = (behind >= 0) & (behind < chips)
    rows = keep_ref.shape[0] // pieces
    cols = out_ref.shape[1]
    third = cols - side
    far_at = pl.multiple_of(odd * (side + cols), FB)
    near_at = pl.multiple_of((1 - odd) * (side + cols), FB)

    def cut(i):
        return pl.ds(i * rows, rows)

    def to_mate(i):
        return remote(give_ref.at[cut(i)], mate_buf.at[cut(i)], mate_s.at[i], mate_r.at[i], chip, 1 - core)

    def to_far(i):
        return remote(far_out.at[cut(i)], far_in.at[cut(i)], far_s.at[i], far_r.at[i], behind, core)

    own_at = pl.ds(pl.multiple_of(odd * side, FB), third)
    sum_at = pl.ds(pl.multiple_of((1 - odd) * third, FB), side)
    got_own = pl.ds(pl.multiple_of((1 - odd) * side, FB), third)
    got_sum = pl.ds(pl.multiple_of(odd * third, FB), side)

    def load(i):
        return pltpu.make_async_copy(keep_ref.at[cut(i)], total.at[cut(i)], load_s.at[i])

    def own_near(i, cols_at):
        return remote(
            near_out.at[cut(i), cols_at], near_in.at[cut(i), cols_at],
            near_s.at[i], near_r.at[i], partner, core,
        )

    def sum_near(i, cols_at):
        return remote(
            near_out.at[cut(i), cols_at], near_in.at[cut(i), cols_at],
            near_s.at[pieces + i], near_r.at[pieces + i], partner, core,
        )

    for i in range(pieces):
        load(i).start()
    greet([
        (True, chip, 1 - core), (True, partner, core),
        (has_ahead, ahead, core), (has_behind, behind, core),
    ])
    for i in range(pieces):
        to_mate(i).start()
    for i in range(pieces):
        load(i).wait()
        to_mate(i).wait_recv()
        total[cut(i), :] = total[cut(i), :] + mate_buf[cut(i), :].astype(f32)
        far_out[cut(i), :] = total[cut(i), pl.ds(far_at, side)].astype(bf16)

        @pl.when(has_behind)
        def _():
            to_far(i).start()

        mine_at = pl.multiple_of(near_at + odd * third, FB)
        near_out[cut(i), own_at] = total[cut(i), pl.ds(mine_at, third)].astype(bf16)
        own_near(i, own_at).start()

    for i in range(pieces):
        @pl.when(has_ahead)
        def _():
            to_far(i).wait_recv()

        mine_at = pl.multiple_of(near_at + (1 - odd) * third, FB)
        mine = total[cut(i), pl.ds(mine_at, third)]
        theirs = jnp.where(has_ahead, far_in[cut(i), :].astype(f32), 0.0)
        blank = jnp.zeros_like(mine)
        mine = jnp.where(
            odd == 0,
            jnp.concatenate([mine, blank], axis=1),
            jnp.concatenate([blank, mine], axis=1),
        )
        near_out[cut(i), sum_at] = (mine + theirs).astype(bf16)
        sum_near(i, sum_at).start()

    for i in range(pieces):
        own_near(i, got_own).wait_recv()
        sum_near(i, got_sum).wait_recv()
        out_ref[cut(i), :] = total[cut(i), side:side + cols] + near_in[cut(i), :].astype(f32)

    for i in range(pieces):
        to_mate(i).wait_send()
        own_near(i, own_at).wait_send()
        sum_near(i, sum_at).wait_send()

        @pl.when(has_behind)
        def _():
            to_far(i).wait_send()


def on_device(
    basis_values, density, sig_blocks, grid_weights, atom_of, in_weight, in_bias,
    atom_proj, hidden_weight, atom_in, hidden_bias, out_weight,
):
    chips, cores = lax.axis_size("pts"), lax.axis_size("blk")
    batches, points, sig = basis_values.shape
    rows, cols = density.shape
    own_blocks = rows // FB
    chip_funcs = rows * cores
    hid = in_weight.shape[0]
    width = atom_proj.shape[1]
    count = 3 * ATOM_DEV * cores
    side = 2 * chip_funcs
    hbm = pl.BlockSpec(memory_space=pl.ANY)
    dma = pltpu.SemaphoreType.DMA

    def talk(number):
        return pltpu.CompilerParams(
            collective_id=number, has_side_effects=True, vmem_limit_bytes=60 * 1024 * 1024
        )

    pieces = 4
    turn_pts = min(1024, points)
    turns = points // turn_pts

    def gather_body(*refs):
        gather_kernel(chips, side, pieces, *refs)

    vt, mate, near_mine, near_mate, far_mine, far_mate = pl.pallas_call(
        gather_body,
        grid=(batches * turns,),
        in_specs=[hbm, pl.BlockSpec((1, turn_pts, sig), lambda g: (g // turns, g % turns, 0))],
        out_specs=[pl.BlockSpec((1, sig, turn_pts), lambda g: (g // turns, 0, g % turns))] + [hbm] * 5,
        out_shape=[jax.ShapeDtypeStruct((batches, sig, points), bf16)]
        + [jax.ShapeDtypeStruct((rows, cols), bf16)] * 3
        + [jax.ShapeDtypeStruct((rows, side), bf16)] * 2,
        scratch_shapes=[dma((pieces + 1,)), dma((pieces + 1,)), dma, dma]
        + [dma((pieces,))] * 2 + [dma((pieces + 1,))] * 2 + [dma((pieces,))] * 2,
        compiler_params=talk(0),
        name="gather_density",
    )(density, basis_values)

    block_pts = min(2048, points)
    step_pts = min(512, block_pts)
    grid = (batches, points // block_pts)
    flat = pl.BlockSpec((batches, block_pts), lambda b, i: (0, i))
    vt_spec = pl.BlockSpec((1, sig, block_pts), lambda b, i: (b, 0, i))
    hid_spec = pl.BlockSpec((1, hid, block_pts), lambda b, i: (b, 0, i))
    limit = pltpu.CompilerParams(vmem_limit_bytes=60 * 1024 * 1024)

    def first_body(*refs):
        first_kernel(step_pts, own_blocks, cores, *refs)

    hidden, sums = pl.pallas_call(
        first_body,
        grid=grid,
        in_specs=[SMALL] + [WHOLE] * 6
        + [vt_spec, flat, flat]
        + [WHOLE] * 3,
        out_specs=[hid_spec, WHOLE],
        out_shape=[
            jax.ShapeDtypeStruct((batches, hid, points), bf16),
            jax.ShapeDtypeStruct((count, 2 * width), f32),
        ],
        scratch_shapes=[
            pltpu.VMEM((sig, sig), bf16),
            pltpu.VMEM((2 * count, hid), f32),
            pltpu.VMEM((count, FB), f32),
        ],
        compiler_params=limit,
        name="first_pass",
    )(
        sig_blocks, density, mate, near_mine, near_mate, far_mine, far_mate,
        vt, grid_weights, atom_of, in_weight[None, :], in_bias[None, :], atom_proj.T,
    )

    def atoms_body(*refs):
        atoms_kernel(chips, cores, *refs)

    near = pl.pallas_call(
        atoms_body,
        in_specs=[WHOLE],
        out_specs=WHOLE,
        out_shape=jax.ShapeDtypeStruct(sums.shape, f32),
        scratch_shapes=[pltpu.VMEM((9,) + sums.shape, f32), dma((9,)), dma((9,))],
        compiler_params=talk(1),
        name="atom_exchange",
    )(sums)

    def second_body(*refs):
        second_kernel(step_pts, own_blocks, cores, *refs)

    packed = cols + 4 * chip_funcs
    keep, give = pl.pallas_call(
        second_body,
        grid=grid,
        in_specs=[SMALL, WHOLE, pl.BlockSpec((1, block_pts, sig), lambda b, i: (b, i, 0))]
        + [vt_spec, hid_spec, flat, flat] + [WHOLE] * 4,
        out_specs=[WHOLE, WHOLE],
        out_shape=[
            jax.ShapeDtypeStruct((rows, packed), f32),
            jax.ShapeDtypeStruct((rows, packed), bf16),
        ],
        scratch_shapes=[
            pltpu.VMEM((hid, 2 * count), bf16),
            pltpu.VMEM((hid, hid), bf16),
            pltpu.VMEM((sig, sig), f32),
            pltpu.VMEM((cores, rows, packed), f32),
            pltpu.VMEM((sig, block_pts), bf16),
        ],
        compiler_params=limit,
        name="second_pass",
    )(
        sig_blocks, near, basis_values, vt, hidden, grid_weights, atom_of, atom_in, hidden_weight,
        hidden_bias[None, :], out_weight[None, :],
    )

    def scatter_body(*refs):
        scatter_kernel(chips, side, pieces, *refs)

    return pl.pallas_call(
        scatter_body,
        in_specs=[hbm, hbm],
        out_specs=WHOLE,
        out_shape=jax.ShapeDtypeStruct((rows, cols), f32),
        scratch_shapes=[
            pltpu.VMEM((rows, packed), bf16),
            pltpu.VMEM((rows, packed), f32),
            pltpu.VMEM((rows, side), bf16),
            pltpu.VMEM((rows, side), bf16),
            pltpu.VMEM((rows, cols), bf16),
            pltpu.VMEM((rows, cols), bf16),
        ] + [dma((pieces,))] * 4 + [dma((2 * pieces,))] * 2 + [dma((pieces,))],
        compiler_params=talk(2),
        name="scatter_terms",
    )(keep, give)


def solution(mesh):
    split = ("pts", "blk")
    return jax.shard_map(
        on_device,
        mesh=mesh,
        in_specs=(
            P(split, None, None), P(split, None), P(split, None), P(split, None), P(split, None),
            P(), P(), P(), P(), P(), P(), P(),
        ),
        out_specs=P(split, None),
        check_vma=False,
    )
```

```python
import jax
import jax.numpy as jnp
from jax import lax
from jax.experimental import pallas as pl
from jax.experimental.pallas import tpu as pltpu
from jax.sharding import PartitionSpec as P

FB = 128
ATOM_DEV = 16
eps_atom = 0.0001
f32 = jnp.float32
bf16 = jnp.bfloat16
NT = (((1,), (1,)), ((), ()))
WHOLE = pl.BlockSpec(memory_space=pltpu.VMEM)
SMALL = pl.BlockSpec(memory_space=pltpu.SMEM)


def column(row):
    return jnp.broadcast_to(row, (FB, row.shape[1])).T[:, 0:1]


def silu_of_double(half):
    return half + half * jnp.tanh(half)


def members(atoms, first, count):
    ids = lax.broadcasted_iota(jnp.int32, (count, atoms.shape[1]), 0) + first
    return ids == atoms


def first_kernel(
    step_pts, own_blocks, cores,
    sig_ref, mine_ref, mate_ref, near_mine, near_mate, far_mine, far_mate,
    vt_ref, w_ref, atom_ref, win_ref, bin_ref, proj_ref,
    hid_ref, sums_ref,
    sub_ref, seg_ref, sq_ref,
):
    batch, step = pl.program_id(0), pl.program_id(1)
    chip, core = lax.axis_index("pts"), lax.axis_index("blk")
    chip_blocks = own_blocks * cores
    count = sq_ref.shape[0]
    sig = sub_ref.shape[0] // FB
    odd = chip % 2

    @pl.when(step == 0)
    def _():
        for r in range(sig):
            rb = sig_ref[batch, r] - chip_blocks * (chip - 1)
            r_chip, r_in = rb // chip_blocks, rb % chip_blocks
            is_mine = (r_in // own_blocks) == core
            rows = pl.ds(pl.multiple_of((r_in % own_blocks) * FB, FB), FB)
            for s in range(sig):
                cb = sig_ref[batch, s] - chip_blocks * (chip - 1)
                c_chip = cb // chip_blocks
                near_at = jnp.clip(cb + chip_blocks * (2 * odd - 1), 0, 3 * chip_blocks - 1)
                far_at = jnp.clip(cb - chip_blocks * odd, 0, 2 * chip_blocks - 1)
                mid = pl.ds(pl.multiple_of(cb * FB, FB), FB)
                near = pl.ds(pl.multiple_of(near_at * FB, FB), FB)
                far = pl.ds(pl.multiple_of(far_at * FB, FB), FB)
                block = jnp.where(
                    r_chip == 1,
                    jnp.where(is_mine, mine_ref[rows, mid], mate_ref[rows, mid]),
                    jnp.where(
                        r_chip == 2 - 2 * odd,
                        jnp.where(is_mine, near_mine[rows, near], near_mate[rows, near]),
                        jnp.where(is_mine, far_mine[rows, far], far_mate[rows, far]),
                    ),
                )
                inside = jnp.abs(c_chip - r_chip) <= 1
                block = jnp.where(inside, block, jnp.zeros_like(block))
                sub_ref[s * FB:(s + 1) * FB, r * FB:(r + 1) * FB] = block.T
        half = sub_ref.shape[0] // 2
        folded = sub_ref[0:half, half:].astype(f32) + sub_ref[half:, 0:half].astype(f32).T
        sub_ref[0:half, half:] = folded.astype(bf16)

    @pl.when((step == 0) & (batch == 0))
    def _():
        seg_ref[...] = jnp.zeros_like(seg_ref)
        sq_ref[...] = jnp.zeros_like(sq_ref)

    w_in, b_in = column(0.5 * win_ref[...]), column(0.5 * bin_ref[...])
    first = (chip - 1) * (count // 3)
    for at in range(0, vt_ref.shape[2], step_pts):
        pts = pl.ds(at, step_pts)
        vt = vt_ref[0, :, pts]
        half = sub_ref.shape[0] // 2
        mixed = jnp.dot(sub_ref[0:half, :], vt, preferred_element_type=f32)
        rho = jnp.sum(mixed * vt[0:half].astype(f32), axis=0, keepdims=True)
        mixed = jnp.dot(sub_ref[half:, half:], vt[half:], preferred_element_type=f32)
        rho = rho + jnp.sum(mixed * vt[half:].astype(f32), axis=0, keepdims=True)
        hidden = silu_of_double(w_in * rho + b_in).astype(bf16)
        hid_ref[0, :, pts] = hidden
        weights = w_ref[pl.ds(batch, 1), pts]
        member = members(atom_ref[pl.ds(batch, 1), pts], first, count)
        held = jnp.where(member, jnp.broadcast_to(weights, member.shape), 0.0)
        high = held.astype(bf16)
        low = (held - high.astype(f32)).astype(bf16)
        both = jnp.concatenate([high, low], axis=0)
        seg_ref[...] += lax.dot_general(both, hidden, NT, preferred_element_type=f32)
        squares = held * held
        part = squares[:, 0:FB]
        for k in range(FB, step_pts, FB):
            part = part + squares[:, k:k + FB]
        sq_ref[...] += part

    @pl.when((step == pl.num_programs(1) - 1) & (batch == pl.num_programs(0) - 1))
    def _():
        total = seg_ref[0:count, :] + seg_ref[count:, :]
        top = total.astype(bf16)
        rest = total - top.astype(f32)
        mid = rest.astype(bf16)
        last = (rest - mid.astype(f32)).astype(bf16)
        sums = jnp.zeros((count, proj_ref.shape[0]), f32)
        for part in (last, mid, top):
            sums = sums + lax.dot_general(part, proj_ref[...], NT, preferred_element_type=f32)
        squares = jnp.sum(sq_ref[...], axis=1, keepdims=True)
        width = sums_ref.shape[1] - sums.shape[1]
        sums_ref[...] = jnp.concatenate([sums, jnp.broadcast_to(squares, (count, width))], axis=1)


def second_kernel(
    step_pts, own_blocks, cores,
    sig_ref, near_ref, v_ref, vt_ref, hid_ref, w_ref, atom_ref, atin_ref, hw_ref, hb_ref, ow_ref,
    keep_ref, give_ref,
    hwt_ref, bm_ref, acc_ref, wt_ref,
):
    batch, step = pl.program_id(0), pl.program_id(1)
    chip, core = lax.axis_index("pts"), lax.axis_index("blk")
    chip_blocks = own_blocks * cores
    count = near_ref.shape[0]
    width = atin_ref.shape[0]
    sig = bm_ref.shape[0] // FB

    @pl.when((step == 0) & (batch == 0))
    def _():
        squares = near_ref[:, width:width + 1]
        feature = (near_ref[:, 0:width] / jnp.sqrt(squares + eps_atom)).astype(bf16)
        table = jnp.dot(feature, atin_ref[...], preferred_element_type=f32)
        high = table.astype(bf16)
        low = (table - high.astype(f32)).astype(bf16)
        spare = hwt_ref.shape[1] - hw_ref.shape[0] - 2 * count
        blank = jnp.zeros((spare, hw_ref.shape[1]), f32)
        stack = [hw_ref[...].astype(f32), high.astype(f32), low.astype(f32), blank]
        hwt_ref[...] = (0.5 * jnp.concatenate(stack, axis=0)).T.astype(bf16)
        acc_ref[...] = jnp.zeros_like(acc_ref)

    @pl.when(step == 0)
    def _():
        bm_ref[...] = jnp.zeros_like(bm_ref)

    weights = ow_ref[...].astype(f32)
    weights = jnp.concatenate([weights[k:k + 1, :] for k in range(weights.shape[0])], axis=1)
    hb, ow = column(0.5 * hb_ref[...]), column(weights)
    spare = hwt_ref.shape[1] - hid_ref.shape[1] - 2 * count
    first = (chip - 1) * (count // 3)
    for at in range(0, vt_ref.shape[2], step_pts):
        pts = pl.ds(at, step_pts)
        member = members(atom_ref[pl.ds(batch, 1), pts], first, count)
        member = jnp.where(member, 1.0, 0.0).astype(bf16)
        blank = jnp.zeros((spare, step_pts), bf16)
        both = jnp.concatenate([hid_ref[0, :, pts], member, member, blank], axis=0)
        before = jnp.dot(hwt_ref[...], both, preferred_element_type=f32) + hb
        second = silu_of_double(before).astype(bf16).astype(f32)
        point = jnp.sum(second * ow, axis=0, keepdims=True)
        scale = w_ref[pl.ds(batch, 1), pts] * point
        vt = vt_ref[0, :, pts]
        wt_ref[:, pts] = (scale * vt.astype(f32)).astype(bf16)

    half = bm_ref.shape[0] // 2
    bm_ref[0:half, :] += jnp.dot(wt_ref[0:half, :], v_ref[0], preferred_element_type=f32)
    bm_ref[half:, half:] += jnp.dot(wt_ref[half:, :], v_ref[0, :, half:], preferred_element_type=f32)

    @pl.when(step == pl.num_programs(1) - 1)
    def _():
        bm_ref[half:, 0:half] = bm_ref[0:half, half:].T
        for r in range(sig):
            rb = sig_ref[batch, r] - chip_blocks * (chip - 1)
            r_chip, r_in = rb // chip_blocks, rb % chip_blocks
            r_core = r_in // own_blocks
            rows = pl.ds(pl.multiple_of((r_in % own_blocks) * FB, FB), FB)
            base = jnp.where(r_chip == 0, 0, jnp.where(r_chip == 1, 2 * chip_blocks, 4 * chip_blocks))
            for s in range(sig):
                cb = sig_ref[batch, s] - chip_blocks * (chip - 1)
                inside = jnp.abs(cb // chip_blocks - r_chip) <= 1

                @pl.when(inside)
                def _():
                    cols = pl.ds(pl.multiple_of((base + cb) * FB, FB), FB)
                    acc_ref[r_core, rows, cols] += bm_ref[r * FB:(r + 1) * FB, s * FB:(s + 1) * FB]

    @pl.when((step == pl.num_programs(1) - 1) & (batch == pl.num_programs(0) - 1))
    def _():
        keep_ref[...] = acc_ref[core]
        give_ref[...] = acc_ref[1 - core].astype(bf16)


def remote(src, dst, send, recv, chip, core):
    return pltpu.make_async_remote_copy(
        src_ref=src, dst_ref=dst, send_sem=send, recv_sem=recv,
        device_id=(chip, core), device_id_type=pl.DeviceIdType.MESH,
    )


def greet(peers):
    barrier = pltpu.get_barrier_semaphore()
    for exists, chip, core in peers:
        @pl.when(exists)
        def _():
            pl.semaphore_signal(
                barrier, inc=1, device_id=(chip, core), device_id_type=pl.DeviceIdType.MESH
            )
    pl.semaphore_wait(barrier, sum(jnp.where(exists, 1, 0) for exists, _, _ in peers))


def gather_kernel(
    chips, side, pieces,
    dens_ref, v_ref,
    vt_ref, mate_ref, near_ref, near_mate, far_ref, far_mate,
    near_s, near_r, mate_s, mate_r, relay_s, relay_r, fwd_s, fwd_r, last_s, last_r,
):
    step, steps = pl.program_id(0), pl.num_programs(0)
    chip, core = lax.axis_index("pts"), lax.axis_index("blk")
    odd = chip % 2
    partner = chip + 1 - 2 * odd
    ahead = chip + 2 - 4 * odd
    behind = chip - 2 + 4 * odd
    has_ahead = (ahead >= 0) & (ahead < chips)
    has_behind = (behind >= 0) & (behind < chips)
    rows = dens_ref.shape[0] // pieces
    third = near_ref.shape[1] - side
    mine_part = pl.ds(pl.multiple_of(odd * third, FB), side)
    mine_rest = pl.ds(pl.multiple_of((1 - odd) * side, FB), third)
    part = pl.ds(pl.multiple_of((1 - odd) * third, FB), side)
    rest = pl.ds(pl.multiple_of(odd * side, FB), third)

    def cut(i):
        return pl.ds(i * rows, rows)

    def to_near(i):
        return remote(
            dens_ref.at[cut(i), mine_part], near_ref.at[cut(i), mine_part],
            near_s.at[i], near_r.at[i], partner, core,
        )

    def from_near(i):
        return remote(
            dens_ref.at[cut(i), part], near_ref.at[cut(i), part],
            near_s.at[i], near_r.at[i], partner, core,
        )

    def rest_near():
        return remote(
            dens_ref.at[:, mine_rest], near_ref.at[:, mine_rest],
            near_s.at[pieces], near_r.at[pieces], partner, core,
        )

    def rest_from():
        return remote(
            dens_ref.at[:, rest], near_ref.at[:, rest],
            near_s.at[pieces], near_r.at[pieces], partner, core,
        )

    def to_mate():
        return remote(dens_ref, mate_ref, mate_s, mate_r, chip, 1 - core)

    def relay(i):
        return remote(near_ref.at[cut(i), part], far_ref.at[cut(i)], relay_s.at[i], relay_r.at[i], ahead, core)

    def forward(i):
        return remote(near_ref.at[cut(i), part], near_mate.at[cut(i), part], fwd_s.at[i], fwd_r.at[i], chip, 1 - core)

    def rest_forward():
        return remote(
            near_ref.at[:, rest], near_mate.at[:, rest],
            fwd_s.at[pieces], fwd_r.at[pieces], chip, 1 - core,
        )

    def finish(i):
        return remote(far_ref.at[cut(i)], far_mate.at[cut(i)], last_s.at[i], last_r.at[i], chip, 1 - core)

    @pl.when(step == 0)
    def _():
        greet([
            (True, chip, 1 - core), (True, partner, core),
            (has_ahead, ahead, core), (has_behind, behind, core),
        ])
        for i in range(pieces):
            to_near(i).start()
        rest_near().start()
        to_mate().start()

    vt_ref[0] = v_ref[0].T

    for i in range(pieces):
        @pl.when(step == ((i + 1) * steps) // pieces - 1)
        def _():
            from_near(i).wait_recv()

            @pl.when(has_ahead)
            def _():
                relay(i).start()

            forward(i).start()

    @pl.when(step == steps - 1)
    def _():
        for i in range(pieces):
            @pl.when(has_behind)
            def _():
                relay(i).wait_recv()
                finish(i).start()
        rest_from().wait_recv()
        rest_forward().start()
        to_mate().wait()
        rest_near().wait_send()
        rest_forward().wait()
        for i in range(pieces):
            to_near(i).wait_send()
            forward(i).wait()

            @pl.when(has_ahead)
            def _():
                relay(i).wait_send()

            @pl.when(has_behind)
            def _():
                finish(i).wait()


def atoms_kernel(chips, cores, sums_ref, near_ref, land_ref, send, recv):
    chip, core = lax.axis_index("pts"), lax.axis_index("blk")
    third = sums_ref.shape[0] // 3
    plans = []
    for d in (-1, 1, -2, 2):
        for flip in (0, 1):
            plans.append((d, flip))
    plans.append((0, 1))

    def other(flip):
        return core + flip * (1 - 2 * core)

    def span(d):
        count = 3 - abs(d)
        return max(d, 0), max(-d, 0), count

    def valid(at):
        return (at >= 0) & (at < chips)

    def copy(k, d, flip):
        take, _, count = span(d)
        return remote(
            sums_ref.at[pl.ds(take * third, count * third)],
            land_ref.at[k, pl.ds(0, count * third)],
            send.at[k], recv.at[k], chip + d, other(flip),
        )

    greet([(valid(chip + d), chip + d, other(flip)) for d, flip in plans])
    for k, (d, flip) in enumerate(plans):
        @pl.when(valid(chip + d))
        def _():
            copy(k, d, flip).start()

    near_ref[...] = sums_ref[...]
    for k, (d, flip) in enumerate(plans):
        _, put, count = span(d)

        @pl.when(valid(chip - d))
        def _():
            copy(k, d, flip).wait_recv()
            to = pl.ds(put * third, count * third)
            near_ref[to, :] += land_ref[k, 0:count * third, :]

    for k, (d, flip) in enumerate(plans):
        @pl.when(valid(chip + d))
        def _():
            copy(k, d, flip).wait_send()


def scatter_kernel(
    chips, side, pieces,
    keep_ref, give_ref, own_ref, near_in,
    mate_buf, total, far_out, far_in, near_out,
    mate_s, mate_r, far_s, far_r, near_s, near_r, load_s, save_s,
):
    chip, core = lax.axis_index("pts"), lax.axis_index("blk")
    odd = chip % 2
    partner = chip + 1 - 2 * odd
    ahead = chip + 2 - 4 * odd
    behind = chip - 2 + 4 * odd
    has_ahead = (ahead >= 0) & (ahead < chips)
    has_behind = (behind >= 0) & (behind < chips)
    rows = keep_ref.shape[0] // pieces
    cols = own_ref.shape[1]
    third = cols - side
    far_at = pl.multiple_of(odd * (side + cols), FB)
    near_at = pl.multiple_of((1 - odd) * (side + cols), FB)

    def cut(i):
        return pl.ds(i * rows, rows)

    def to_mate(i):
        return remote(give_ref.at[cut(i)], mate_buf.at[cut(i)], mate_s.at[i], mate_r.at[i], chip, 1 - core)

    def to_far(i):
        return remote(far_out.at[cut(i)], far_in.at[cut(i)], far_s.at[i], far_r.at[i], behind, core)

    own_at = pl.ds(pl.multiple_of(odd * side, FB), third)
    sum_at = pl.ds(pl.multiple_of((1 - odd) * third, FB), side)
    got_own = pl.ds(pl.multiple_of((1 - odd) * side, FB), third)
    got_sum = pl.ds(pl.multiple_of(odd * third, FB), side)

    def load(i):
        return pltpu.make_async_copy(keep_ref.at[cut(i)], total.at[cut(i)], load_s.at[i])

    def save(i):
        return pltpu.make_async_copy(
            total.at[cut(i), pl.ds(side, cols)], own_ref.at[cut(i)], save_s.at[i]
        )

    def own_near(i, cols_at):
        return remote(
            near_out.at[cut(i), cols_at], near_in.at[cut(i), cols_at],
            near_s.at[i], near_r.at[i], partner, core,
        )

    def sum_near(i, cols_at):
        return remote(
            near_out.at[cut(i), cols_at], near_in.at[cut(i), cols_at],
            near_s.at[pieces + i], near_r.at[pieces + i], partner, core,
        )

    for i in range(pieces):
        load(i).start()
    greet([
        (True, chip, 1 - core), (True, partner, core),
        (has_ahead, ahead, core), (has_behind, behind, core),
    ])
    for i in range(pieces):
        to_mate(i).start()
    for i in range(pieces):
        load(i).wait()
        to_mate(i).wait_recv()
        total[cut(i), :] = total[cut(i), :] + mate_buf[cut(i), :].astype(f32)
        far_out[cut(i), :] = total[cut(i), pl.ds(far_at, side)].astype(bf16)

        @pl.when(has_behind)
        def _():
            to_far(i).start()

        save(i).start()
        mine_at = pl.multiple_of(near_at + odd * third, FB)
        near_out[cut(i), own_at] = total[cut(i), pl.ds(mine_at, third)].astype(bf16)
        own_near(i, own_at).start()

    for i in range(pieces):
        @pl.when(has_ahead)
        def _():
            to_far(i).wait_recv()

        mine_at = pl.multiple_of(near_at + (1 - odd) * third, FB)
        mine = total[cut(i), pl.ds(mine_at, third)]
        theirs = jnp.where(has_ahead, far_in[cut(i), :].astype(f32), 0.0)
        blank = jnp.zeros_like(mine)
        mine = jnp.where(
            odd == 0,
            jnp.concatenate([mine, blank], axis=1),
            jnp.concatenate([blank, mine], axis=1),
        )
        near_out[cut(i), sum_at] = (mine + theirs).astype(bf16)
        sum_near(i, sum_at).start()

    for i in range(pieces):
        own_near(i, got_own).wait_recv()
        sum_near(i, got_sum).wait_recv()
        save(i).wait()

    for i in range(pieces):
        to_mate(i).wait_send()
        own_near(i, own_at).wait_send()
        sum_near(i, sum_at).wait_send()

        @pl.when(has_behind)
        def _():
            to_far(i).wait_send()


def on_device(
    basis_values, density, sig_blocks, grid_weights, atom_of, in_weight, in_bias,
    atom_proj, hidden_weight, atom_in, hidden_bias, out_weight,
):
    chips, cores = lax.axis_size("pts"), lax.axis_size("blk")
    batches, points, sig = basis_values.shape
    rows, cols = density.shape
    own_blocks = rows // FB
    chip_funcs = rows * cores
    hid = in_weight.shape[0]
    width = atom_proj.shape[1]
    count = 3 * ATOM_DEV * cores
    side = 2 * chip_funcs
    hbm = pl.BlockSpec(memory_space=pl.ANY)
    dma = pltpu.SemaphoreType.DMA

    def talk(number):
        return pltpu.CompilerParams(
            collective_id=number, has_side_effects=True, vmem_limit_bytes=60 * 1024 * 1024
        )

    pieces = 4
    turn_pts = min(1024, points)
    turns = points // turn_pts

    def gather_body(*refs):
        gather_kernel(chips, side, pieces, *refs)

    vt, mate, near_mine, near_mate, far_mine, far_mate = pl.pallas_call(
        gather_body,
        grid=(batches * turns,),
        in_specs=[hbm, pl.BlockSpec((1, turn_pts, sig), lambda g: (g // turns, g % turns, 0))],
        out_specs=[pl.BlockSpec((1, sig, turn_pts), lambda g: (g // turns, 0, g % turns))] + [hbm] * 5,
        out_shape=[jax.ShapeDtypeStruct((batches, sig, points), bf16)]
        + [jax.ShapeDtypeStruct((rows, cols), bf16)] * 3
        + [jax.ShapeDtypeStruct((rows, side), bf16)] * 2,
        scratch_shapes=[dma((pieces + 1,)), dma((pieces + 1,)), dma, dma]
        + [dma((pieces,))] * 2 + [dma((pieces + 1,))] * 2 + [dma((pieces,))] * 2,
        compiler_params=talk(0),
        name="gather_density",
    )(density, basis_values)

    block_pts = min(2048, points)
    step_pts = min(512, block_pts)
    grid = (batches, points // block_pts)
    flat = pl.BlockSpec((batches, block_pts), lambda b, i: (0, i))
    vt_spec = pl.BlockSpec((1, sig, block_pts), lambda b, i: (b, 0, i))
    hid_spec = pl.BlockSpec((1, hid, block_pts), lambda b, i: (b, 0, i))
    limit = pltpu.CompilerParams(vmem_limit_bytes=60 * 1024 * 1024)

    def first_body(*refs):
        first_kernel(2 * step_pts, own_blocks, cores, *refs)

    hidden, sums = pl.pallas_call(
        first_body,
        grid=grid,
        in_specs=[SMALL] + [WHOLE] * 6
        + [vt_spec, flat, flat]
        + [WHOLE] * 3,
        out_specs=[hid_spec, WHOLE],
        out_shape=[
            jax.ShapeDtypeStruct((batches, hid, points), bf16),
            jax.ShapeDtypeStruct((count, 2 * width), f32),
        ],
        scratch_shapes=[
            pltpu.VMEM((sig, sig), bf16),
            pltpu.VMEM((2 * count, hid), f32),
            pltpu.VMEM((count, FB), f32),
        ],
        compiler_params=limit,
        name="first_pass",
    )(
        sig_blocks, density, mate, near_mine, near_mate, far_mine, far_mate,
        vt, grid_weights, atom_of, in_weight[None, :], in_bias[None, :], atom_proj.T,
    )

    def atoms_body(*refs):
        atoms_kernel(chips, cores, *refs)

    near = pl.pallas_call(
        atoms_body,
        in_specs=[WHOLE],
        out_specs=WHOLE,
        out_shape=jax.ShapeDtypeStruct(sums.shape, f32),
        scratch_shapes=[pltpu.VMEM((9,) + sums.shape, f32), dma((9,)), dma((9,))],
        compiler_params=talk(1),
        name="atom_exchange",
    )(sums)

    def second_body(*refs):
        second_kernel(step_pts, own_blocks, cores, *refs)

    packed = cols + 4 * chip_funcs
    keep, give = pl.pallas_call(
        second_body,
        grid=grid,
        in_specs=[SMALL, WHOLE, pl.BlockSpec((1, block_pts, sig), lambda b, i: (b, i, 0))]
        + [vt_spec, hid_spec, flat, flat] + [WHOLE] * 4,
        out_specs=[WHOLE, WHOLE],
        out_shape=[
            jax.ShapeDtypeStruct((rows, packed), f32),
            jax.ShapeDtypeStruct((rows, packed), bf16),
        ],
        scratch_shapes=[
            pltpu.VMEM((hid, 2 * FB * pl.cdiv(hid + 2 * count, 2 * FB)), bf16),
            pltpu.VMEM((sig, sig), f32),
            pltpu.VMEM((cores, rows, packed), f32),
            pltpu.VMEM((sig, block_pts), bf16),
        ],
        compiler_params=limit,
        name="second_pass",
    )(
        sig_blocks, near, basis_values, vt, hidden, grid_weights, atom_of, atom_in, hidden_weight,
        hidden_bias[None, :], out_weight.reshape(-1, FB),
    )

    def scatter_body(*refs):
        scatter_kernel(chips, side, pieces, *refs)

    own_terms, near_terms = pl.pallas_call(
        scatter_body,
        in_specs=[hbm, hbm],
        out_specs=[hbm, hbm],
        out_shape=[
            jax.ShapeDtypeStruct((rows, cols), f32),
            jax.ShapeDtypeStruct((rows, cols), bf16),
        ],
        scratch_shapes=[
            pltpu.VMEM((rows, packed), bf16),
            pltpu.VMEM((rows, packed), f32),
            pltpu.VMEM((rows, side), bf16),
            pltpu.VMEM((rows, side), bf16),
            pltpu.VMEM((rows, cols), bf16),
        ] + [dma((pieces,))] * 4 + [dma((2 * pieces,))] * 2 + [dma((pieces,))] * 2,
        compiler_params=talk(2),
        name="scatter_terms",
    )(keep, give)
    return own_terms + near_terms.astype(f32)


def solution(mesh):
    split = ("pts", "blk")
    return jax.shard_map(
        on_device,
        mesh=mesh,
        in_specs=(
            P(split, None, None), P(split, None), P(split, None), P(split, None), P(split, None),
            P(), P(), P(), P(), P(), P(), P(),
        ),
        out_specs=P(split, None),
        check_vma=False,
    )
```
